512 devices in a mesh: blk: 32 (over z, y_lo), rep: 16 (over x, y_hi, core).
Axes of the slice: x: 4, y: 4 (y_hi: 2, y_lo: 2; y = y_hi * 2 + y_lo), z: 16, core: 2. Of those that a mesh axis runs over, the one named last changes fastest.
Arguments:
- users: bfloat16 [524288, 128], P(('blk', 'rep')), may hold values from -2 to 2
- items: bfloat16 [32768, 128], P('blk'), may hold values from -2 to 2
- ratings: bfloat16 [32, 16, 3, 40, 128, 128], P('blk', 'rep'), may hold values from 0 to 4
- user_tiles: int32 [32, 16, 3, 40], P('blk', 'rep'), may hold values from 0 to 7
- item_tiles: int32 [32, 16, 3, 40], P('blk', 'rep'), may hold values from 0 to 7
- counts: int32 [32, 16, 3], P('blk', 'rep'), may hold values from 5 to 40, as said below
Outputs:
- user_new: bfloat16 [524288, 128], P(('blk', 'rep'))
- item_new: bfloat16 [32768, 128], P('blk')
The draws below stay inside these ranges and needn't reach their ends.
Inputs may be any that keep to these rules, and one draw needn't show every extreme that they name: `counts`: each device and stop has between 5 and 40 live slots, the first ones of its list; some device has all 40 live for some stop.
All inputs are finite; a program needn't handle non-finite values.
Results may differ from the reference program's by a relative error of at most 0.0033.
Values may be sent and summed in bfloat16 or wider, within the bound.
A program may use at most 64 MiB of HBM per device.

```python
import math
import jax
import jax.numpy as jnp
from jax import lax

K = 128
TILE = 128
USER_DEV = 1024
ITEM_BLK = 1024
STOPS = 3
TILE_SLOTS = 40
USERS = 524288
ITEMS = 32768
N_BLK = 32
N_REP = 16


def draw_counts(key, part):
    grid_shape = (N_BLK, N_REP, STOPS)
    loaded = jax.random.randint(jax.random.fold_in(key, 11), grid_shape, 0, 8) == 0
    baseline = jax.random.randint(jax.random.fold_in(key, 12), grid_shape, max(TILE_SLOTS // 8, 1), TILE_SLOTS // 2 + 1)
    filled = jnp.where(loaded, TILE_SLOTS, baseline).astype(jnp.int32)
    chosen = jax.random.randint(jax.random.fold_in(key, 13), (), 0, N_BLK * N_REP * STOPS)
    flattened = filled.reshape(-1).at[chosen].set(TILE_SLOTS)
    return flattened.reshape(grid_shape).astype(jnp.int32)


def place_ends(result, rng, least, top_value):
    longest = result.shape.index(max(result.shape))
    spots = []
    for shift in (0, 1):
        where = [jax.random.randint(jax.random.fold_in(rng, axis), (), 0, length) for axis, length in enumerate(result.shape)]
        where[longest] = (where[longest] + shift) % result.shape[longest]
        spots.append(tuple(where))
    return result.at[spots[0]].set(least).at[spots[1]].set(top_value)


def shard_levels(stream_key, shape, split, least, top_value):
    factor_of = 1.0
    for position, parts in split:
        steps = jax.random.uniform(jax.random.fold_in(jax.random.fold_in(stream_key, 6), position), (parts,), jnp.float32, least / len(split), top_value / len(split))
        factor_of = factor_of * jnp.repeat(jnp.exp(steps), shape[position] // parts).reshape((-1,) + (1,) * (len(shape) - 1 - position))
    return factor_of


def scatter_about(rng, dims, scale, bound, split=(), held_as=jnp.bfloat16):
    drawn = jax.random.normal(rng, dims, jnp.float32) * scale
    if len(split) > 0:
        drawn = shard_levels(rng, dims, split, -0.22, 0.18) * drawn
    return jnp.clip(drawn, min=-bound, max=bound).astype(held_as)


def setup_inputs(seed: int = 0) -> dict:
    streams_of = jax.random.split(jax.random.key(seed), 7)
    return {
        "users": scatter_about(streams_of[0], (USERS, K), 0.3, 2.0, ((0, 512),)),
        "items": scatter_about(streams_of[1], (ITEMS, K), 0.3, 2.0, ((0, 32),)),
        "ratings": jnp.clip(4.0 * jax.random.uniform(streams_of[2], (N_BLK, N_REP, STOPS, TILE_SLOTS, TILE, TILE), jnp.float32) ** shard_levels(streams_of[2], (N_BLK, N_REP, STOPS, TILE_SLOTS, TILE, TILE), ((0, 32), (1, 16)), -0.2, 0.2), 0.0, 4.0).astype(jnp.bfloat16),
        "user_tiles": place_ends(jax.random.randint(streams_of[3], (N_BLK, N_REP, STOPS, TILE_SLOTS), 0, USER_DEV // TILE), jax.random.fold_in(streams_of[3], 1), 0, (USER_DEV // TILE) - 1).astype(jnp.int32),
        "item_tiles": place_ends(jax.random.randint(streams_of[4], (N_BLK, N_REP, STOPS, TILE_SLOTS), 0, ITEM_BLK // TILE), jax.random.fold_in(streams_of[4], 1), 0, (ITEM_BLK // TILE) - 1).astype(jnp.int32),
        "counts": draw_counts(jax.random.fold_in(streams_of[6], 71), 0),
    }


confidence = 0.5
shrinkage = 0.05
step_gain = 0.3

def slot_terms(user_block, item_block, user_pick, item_pick, rating_tiles, live_count):
    slot_ids = jnp.arange(TILE_SLOTS)
    valid_slots = (slot_ids < live_count).astype(jnp.float32)
    user_rows = user_block[user_pick]
    item_rows = item_block[item_pick]
    predicted = jnp.einsum('gak,gbk->gab', user_rows, item_rows, precision=lax.Precision.HIGHEST)
    rating_vals = rating_tiles.astype(jnp.float32)
    residual = (1.0 + confidence * rating_vals) * (rating_vals - predicted) * valid_slots[:, None, None]
    residual = lax.optimization_barrier(residual.astype(jnp.bfloat16)).astype(jnp.float32)
    user_terms = jnp.einsum('gab,gbk->gak', residual, item_rows, precision=lax.Precision.HIGHEST)
    item_terms = jnp.einsum('gab,gak->gbk', residual, user_rows, precision=lax.Precision.HIGHEST)
    user_grad = jnp.zeros(user_block.shape, jnp.float32).at[user_pick].add(user_terms)
    item_grad = jnp.zeros(item_block.shape, jnp.float32).at[item_pick].add(item_terms)
    return (user_grad, item_grad)

def reference(users, items, ratings, user_tiles, item_tiles, counts):
    user_count = USER_DEV // TILE
    item_count = ITEM_BLK // TILE
    user_blocks = users.astype(jnp.float32).reshape(N_BLK, N_REP, user_count, TILE, K)
    item_blocks = items.astype(jnp.float32).reshape(N_BLK, item_count, TILE, K)

    def column(block_index):
        column_users = user_blocks[block_index]
        grad_user = jnp.zeros((N_REP, user_count, TILE, K), jnp.float32)
        stop_parts = []
        for station in range(STOPS):
            item_block = item_blocks[(block_index + station) % N_BLK]
            user_grad, item_grad = jax.vmap(slot_terms, in_axes=(0, None, 0, 0, 0, 0))(column_users, item_block, user_tiles[block_index, :, station], item_tiles[block_index, :, station], ratings[block_index, :, station], counts[block_index, :, station])
            grad_user = grad_user + user_grad
            stop_parts.append(lax.optimization_barrier(jnp.sum(item_grad, axis=0)))
        return (grad_user, jnp.stack(stop_parts))
    grad_user, item_parts = lax.map(column, jnp.arange(N_BLK, dtype=jnp.int32))
    grad_item = jnp.zeros((N_BLK, item_count, TILE, K), jnp.float32)
    for station in range(STOPS):
        grad_item = grad_item + jnp.roll(item_parts[:, station], station, axis=0)
    rate_user = step_gain / math.sqrt(STOPS * TILE_SLOTS * TILE * TILE / USER_DEV)
    rate_item = step_gain / math.sqrt(N_REP * STOPS * TILE_SLOTS * TILE * TILE / ITEM_BLK)
    users32 = users.astype(jnp.float32)
    items32 = items.astype(jnp.float32)
    user_new = users32 - rate_user * (grad_user.reshape(users.shape) + shrinkage * users32)
    item_new = items32 - rate_item * (grad_item.reshape(items.shape) + shrinkage * items32)
    return (user_new.astype(jnp.bfloat16), item_new.astype(jnp.bfloat16))
```

```python
import functools
import math

import jax
import jax.numpy as jnp
from jax import lax
from jax.experimental import pallas as pl
from jax.experimental.pallas import tpu as pltpu
from jax.sharding import PartitionSpec as P

CONFIDENCE = 0.5
SHRINKAGE = 0.05
STEP_GAIN = 0.3
GROUP = 20
MESH = pl.DeviceIdType.MESH
F32 = jnp.float32
BF16 = jnp.bfloat16
ORDER = (0, 2, 1)


def kernel(
    rate_user,
    rate_item,
    tab,
    users_hbm,
    items_hbm,
    ratings_hbm,
    user_out,
    item_out,
    users,
    block_0,
    block_1,
    block_2,
    flipped,
    rbuf,
    sums_user,
    sums_item,
    half_out,
    half_in,
    chip_sum,
    pieces,
    fwd_out,
    fwd_in,
    unew,
    inew,
    load_sem,
    fetch_sem,
    swap_sem,
    half_sem,
    piece_sem,
    fwd_sem,
    gather_sem,
    pair_sem,
    out_sem,
):
    blocks = (block_0, block_1, block_2)
    nblk = lax.axis_size("blk")
    nrep = lax.axis_size("rep")
    nq = nrep // 2
    tiles, tile, _ = users.shape
    slots = rbuf.shape[1]
    half = tile // 2
    per = tiles // nq
    quarter = tiles // 4
    b = lax.axis_index("blk")
    r = lax.axis_index("rep")
    yl = b % 2
    q = r // 2
    c = r % 2
    yh = q % 2

    def col(distance):
        return (b + nblk + distance) % nblk

    partner = (b, r + 1 - 2 * c)
    near = b + 1 - 2 * yl
    same = (near, r)
    other = (near, r + 2 - 4 * yh)

    def rating_load(s):
        return pltpu.make_async_copy(ratings_hbm.at[s], rbuf.at[s], load_sem.at[s])

    user_load = pltpu.make_async_copy(users_hbm, users, load_sem.at[3])
    item_load = pltpu.make_async_copy(items_hbm, block_0, load_sem.at[4])
    user_load.start()
    item_load.start()
    for s in ORDER:
        rating_load(s).start()

    barrier = pltpu.get_barrier_semaphore()
    friends = [partner, (col(-2), r), (col(2), r), (col(-1), r), (col(1), r), other]
    friends += [(b, 2 * ((q + d) % nq) + c) for d in range(1, nq)]
    for friend in friends:
        pl.semaphore_signal(barrier, inc=1, device_id=friend, device_id_type=MESH)
    zero = jnp.zeros((tile, tile), F32)
    for s in range(3):
        sums_user[s, slots] = zero
        sums_item[s, slots] = zero
    pl.semaphore_wait(barrier, len(friends))

    def remote(src, dst, sems, i, target):
        return pltpu.make_async_remote_copy(
            src_ref=src,
            dst_ref=dst,
            send_sem=sems.at[0, i],
            recv_sem=sems.at[1, i],
            device_id=target,
            device_id_type=MESH,
        )

    def part(h):
        return pl.ds((2 * c + h) * quarter, quarter)

    def far_copy(h):
        return remote(items_hbm.at[part(h)], block_2.at[part(h)], fetch_sem, h, (col(-2), r))

    def near_copy(h, src):
        return remote(src, block_1.at[part(h)], fetch_sem, 2 + h, other if h else same)

    def swap_copy(s, h):
        view = blocks[s].at[part(h)]
        return remote(view, view, swap_sem, 2 * (s - 1) + h, partner)

    for h in range(2):
        far_copy(h).start()

    @pl.when(yl == 1)
    def _():
        for h in range(2):
            near_copy(h, items_hbm.at[part(h)]).start()

    def compute(s):
        for t in range(tiles):
            flipped[t] = blocks[s][t].T
        count = tab[s, 0, 2 * slots + tiles]

        def body(i, carry):
            base = i * GROUP
            held = []
            for g in range(GROUP):
                k = base + g
                u = users[tab[s, 0, k]]
                it = tab[s, 1, k]
                v = blocks[s][it]
                p = jnp.dot(u, flipped[it], preferred_element_type=F32)
                rating = rbuf[s, k].astype(F32)
                live = (k < count).astype(F32)
                e = ((1.0 + CONFIDENCE * rating) * (rating - p) * live).astype(BF16)
                held.append((k, u, v, e))
            for k, u, v, e in held:
                gu = jnp.dot(e, v, preferred_element_type=F32)
                gi = lax.dot_general(e, u, (((0,), (0,)), ((), ())), preferred_element_type=F32)
                sums_user[s, k] = gu + sums_user[s, tab[s, 0, slots + k]]
                sums_item[s, k] = gi + sums_item[s, tab[s, 1, slots + k]]
            return carry

        lax.fori_loop(0, slots // GROUP, body, 0)

    def half_copy(s):
        return remote(half_out.at[s], half_in.at[s], half_sem, s, partner)

    def send_half(s):
        for t in range(tiles):
            last = tab[s, 1, 2 * slots + t]
            rows = pl.ds(pl.multiple_of((1 - c) * half, half), half)
            half_out[s, t] = sums_item[s, last, rows].astype(BF16)
        half_copy(s).start()

    def piece_copy(s, d):
        target = (q + d) % nq
        return remote(
            chip_sum.at[s, pl.ds(target * per, per)],
            pieces.at[s, d - 1],
            piece_sem,
            s * (nq - 1) + d - 1,
            (b, 2 * target + c),
        )

    def send_pieces(s):
        half_copy(s).wait_recv()
        for t in range(tiles):
            last = tab[s, 1, 2 * slots + t]
            rows = pl.ds(pl.multiple_of(c * half, half), half)
            both = sums_item[s, last, rows] + half_in[s, t].astype(F32)
            chip_sum[s, t] = both.astype(BF16)
        for d in sorted(range(1, nq), key=lambda d: abs(d - nq // 2)):
            piece_copy(s, d).start()

    def column_sum(s):
        for d in range(1, nq):
            piece_copy(s, d).wait_recv()
        total = chip_sum[s, pl.ds(q * per, per)].astype(F32)
        for d in range(1, nq):
            total = total + pieces[s, d - 1].astype(F32)
        return total

    def fwd_copy(s):
        return remote(fwd_out.at[s - 1], fwd_in.at[s - 1], fwd_sem, s - 1, (col(s), r))

    user_load.wait()
    item_load.wait()
    rating_load(0).wait()
    compute(0)
    send_half(0)

    for h in range(2):
        far_copy(h).wait_recv()
        swap_copy(2, h).start()

        @pl.when(yl == 0)
        def _():
            near_copy(h, block_2.at[part(h)]).start()

    send_pieces(0)
    for h in range(2):
        swap_copy(2, h).wait_recv()
    rating_load(2).wait()
    compute(2)
    send_half(2)

    for h in range(2):
        near_copy(h, items_hbm.at[part(h)]).wait_recv()
        swap_copy(1, h).start()
    send_pieces(2)
    for h in range(2):
        swap_copy(1, h).wait_recv()
    rating_load(1).wait()
    compute(1)
    send_half(1)

    for t in range(tiles):
        grad = zero
        for s in ORDER:
            grad = grad + sums_user[s, tab[s, 0, 2 * slots + t]]
        old = users[t].astype(F32)
        unew[t] = (old - rate_user * (grad + SHRINKAGE * old)).astype(BF16)
    user_store = pltpu.make_async_copy(unew, user_out, out_sem.at[0])
    user_store.start()

    send_pieces(1)
    total = column_sum(0)
    for s in (2, 1):
        fwd_out[s - 1] = column_sum(s)
        fwd_copy(s).start()
    for s in (2, 1):
        fwd_copy(s).wait_recv()
        total = total + fwd_in[s - 1]

    mine = pl.ds(q * per, per)
    old = block_0[mine, pl.ds(pl.multiple_of(c * half, half), half)].astype(F32)
    inew[mine, c] = (old - rate_item * (total + SHRINKAGE * old)).astype(BF16)

    def gather_copy(d):
        return remote(
            inew.at[mine, c],
            inew.at[mine, c],
            gather_sem,
            d - 1,
            (b, 2 * ((q + d) % nq) + c),
        )

    def gathered(d):
        view = inew.at[pl.ds(((q + nq - d) % nq) * per, per), c]
        return remote(view, view, gather_sem, d - 1, (b, 2 * ((q + d) % nq) + c))

    def pair_copy(d):
        view = inew.at[pl.ds(((q + nq - d) % nq) * per, per), c]
        return remote(view, view, pair_sem, d, partner)

    def paired(d):
        view = inew.at[pl.ds(((q + nq - d) % nq) * per, per), 1 - c]
        return remote(view, view, pair_sem, d, partner)

    order = sorted(range(1, nq), key=lambda d: abs(d - nq // 2))
    for d in order:
        gather_copy(d).start()
    pair_copy(0).start()
    for d in reversed(order):
        gathered(d).wait_recv()
        pair_copy(d).start()
    for d in range(nq):
        paired(d).wait_recv()
    item_store = pltpu.make_async_copy(inew, item_out, out_sem.at[1])
    item_store.start()

    for h in range(2):
        far_copy(h).wait_send()
        near_copy(h, items_hbm.at[part(h)]).wait_send()
        for s in (1, 2):
            swap_copy(s, h).wait_send()
    for s in ORDER:
        half_copy(s).wait_send()
        for d in range(1, nq):
            piece_copy(s, d).wait_send()
    for s in (1, 2):
        fwd_copy(s).wait_send()
    for d in range(1, nq):
        gather_copy(d).wait_send()
    for d in range(nq):
        pair_copy(d).wait_send()
    user_store.wait()
    item_store.wait()


def slot_table(user_tiles, item_tiles, counts, tiles):
    picks = jnp.stack([user_tiles, item_tiles], axis=1)
    stops, _, slots = picks.shape
    ids = jnp.arange(slots, dtype=jnp.int32)
    every = jnp.broadcast_to(jnp.arange(tiles, dtype=jnp.int32), (stops, 2, tiles))
    wanted = jnp.concatenate([picks, every], axis=2)
    limit = jnp.concatenate([ids, jnp.full((tiles,), slots, jnp.int32)])
    fits = (wanted[..., :, None] == picks[..., None, :]) & (ids[None, :] < limit[:, None])
    found = jnp.max(jnp.where(fits, ids, -1), axis=3)
    found = jnp.where(found < 0, slots, found)
    tail = jnp.broadcast_to(counts[:, None, None], (stops, 2, 1))
    return jnp.concatenate([picks, found, tail], axis=2)


def on_device(users, items, ratings, user_tiles, item_tiles, counts):
    tile = ratings.shape[-1]
    rank = users.shape[1]
    stops, slots = ratings.shape[2:4]
    tiles = users.shape[0] // tile
    half = tile // 2
    nq = lax.axis_size("rep") // 2
    per = tiles // nq
    rate_user = STEP_GAIN / math.sqrt(stops * slots * tile * tile / users.shape[0])
    rate_item = STEP_GAIN / math.sqrt(2 * nq * stops * slots * tile * tile / items.shape[0])
    table = slot_table(user_tiles[0, 0], item_tiles[0, 0], counts[0, 0], tiles)
    anywhere = pl.BlockSpec(memory_space=pl.ANY)
    dma = pltpu.SemaphoreType.DMA
    user_new, item_new = pl.pallas_call(
        functools.partial(kernel, rate_user, rate_item),
        out_shape=(
            jax.ShapeDtypeStruct((tiles, tile, rank), BF16),
            jax.ShapeDtypeStruct((tiles, 2, half, rank), BF16),
        ),
        in_specs=[pl.BlockSpec(memory_space=pltpu.SMEM), anywhere, anywhere, anywhere],
        out_specs=(anywhere, anywhere),
        scratch_shapes=[
            pltpu.VMEM((tiles, tile, rank), BF16),
            pltpu.VMEM((tiles, tile, rank), BF16),
            pltpu.VMEM((tiles, tile, rank), BF16),
            pltpu.VMEM((tiles, tile, rank), BF16),
            pltpu.VMEM((tiles, rank, tile), BF16),
            pltpu.VMEM((stops, slots, tile, tile), BF16),
            pltpu.VMEM((stops, slots + 1, tile, rank), F32),
            pltpu.VMEM((stops, slots + 1, tile, rank), F32),
            pltpu.VMEM((stops, tiles, half, rank), BF16),
            pltpu.VMEM((stops, tiles, half, rank), BF16),
            pltpu.VMEM((stops, tiles, half, rank), BF16),
            pltpu.VMEM((stops, nq - 1, per, half, rank), BF16),
            pltpu.VMEM((2, per, half, rank), F32),
            pltpu.VMEM((2, per, half, rank), F32),
            pltpu.VMEM((tiles, tile, rank), BF16),
            pltpu.VMEM((tiles, 2, half, rank), BF16),
            dma((5,)),
            dma((2, 4)),
            dma((2, 4)),
            dma((2, 3)),
            dma((2, 3 * (nq - 1))),
            dma((2, 2)),
            dma((2, nq - 1)),
            dma((2, nq)),
            dma((2,)),
        ],
        compiler_params=pltpu.CompilerParams(
            collective_id=0, has_side_effects=True, vmem_limit_bytes=67043328
        ),
    )(
        table,
        users.reshape(tiles, tile, rank),
        items.reshape(tiles, tile, rank),
        ratings[0, 0],
    )
    return user_new.reshape(users.shape), item_new.reshape(items.shape)


def solution(mesh):
    return jax.shard_map(
        on_device,
        mesh=mesh,
        in_specs=(
            P(("blk", "rep"), None),
            P("blk", None),
            P("blk", "rep", None, None, None, None),
            P("blk", "rep", None, None),
            P("blk", "rep", None, None),
            P("blk", "rep", None),
        ),
        out_specs=(P(("blk", "rep"), None), P("blk", None)),
        check_vma=False,
    )
```

```python
import functools
import math

import jax
import jax.numpy as jnp
from jax import lax
from jax.experimental import pallas as pl
from jax.experimental.pallas import tpu as pltpu
from jax.sharding import PartitionSpec as P

CONFIDENCE = 0.5
SHRINKAGE = 0.05
STEP_GAIN = 0.3
GROUP = 20
MESH = pl.DeviceIdType.MESH
F32 = jnp.float32
BF16 = jnp.bfloat16
ORDER = (0, 2, 1)


def kernel(
    rate_user,
    rate_item,
    user_tiles_hbm,
    item_tiles_hbm,
    counts_hbm,
    users_hbm,
    items_hbm,
    ratings_hbm,
    user_out,
    item_out,
    users,
    block_0,
    block_1,
    block_2,
    flipped,
    rbuf,
    sums_user,
    sums_item,
    half_out,
    half_in,
    chip_sum,
    pieces,
    fwd_out,
    fwd_in,
    unew,
    inew,
    user_tiles,
    item_tiles,
    counts,
    prev,
    last,
    load_sem,
    fetch_sem,
    swap_sem,
    half_sem,
    piece_sem,
    fwd_sem,
    gather_sem,
    pair_sem,
    out_sem,
):
    blocks = (block_0, block_1, block_2)
    nblk = lax.axis_size("blk")
    nrep = lax.axis_size("rep")
    nq = nrep // 2
    tiles, tile, _ = users.shape
    slots = rbuf.shape[1]
    half = tile // 2
    per = tiles // nq
    quarter = tiles // 4
    b = lax.axis_index("blk")
    r = lax.axis_index("rep")
    yl = b % 2
    q = r // 2
    c = r % 2
    yh = q % 2
    x = q // 2
    nx = nq // 2

    def col(distance):
        return (b + nblk + distance) % nblk

    def target(e):
        return 2 * ((x + e // 2) % nx) + (yh + e) % 2

    def source(e):
        return 2 * ((x + nx - e // 2) % nx) + (yh + e) % 2

    by_distance = sorted(range(1, nq), key=lambda e: (-min(e // 2, nx - e // 2), -(e % 2)))
    partner = (b, r + 1 - 2 * c)
    near = b + 1 - 2 * yl
    same = (near, r)
    other = (near, r + 2 - 4 * yh)

    def rating_load(s):
        return pltpu.make_async_copy(ratings_hbm.at[s], rbuf.at[s], load_sem.at[s])

    user_load = pltpu.make_async_copy(users_hbm, users, load_sem.at[3])
    item_load = pltpu.make_async_copy(items_hbm, block_0, load_sem.at[4])
    small = [(user_tiles_hbm, user_tiles), (item_tiles_hbm, item_tiles), (counts_hbm, counts)]
    small_loads = [
        pltpu.make_async_copy(src, dst, load_sem.at[5 + i]) for i, (src, dst) in enumerate(small)
    ]
    for load in small_loads:
        load.start()
    user_load.start()
    item_load.start()
    for s in ORDER:
        rating_load(s).start()

    barrier = pltpu.get_barrier_semaphore()
    friends = [partner, (col(-2), r), (col(2), r)]
    friends += [(col(s), 2 * target(e) + c) for s in (1, -1) for e in range(nq)]
    friends += [(b, 2 * target(e) + c) for e in range(1, nq)]
    friends += [(b, 2 * target(e) + 1 - c) for e in range(1, nq) if nx > 1 and e // 2 == nx // 2]
    for friend in friends:
        pl.semaphore_signal(barrier, inc=1, device_id=friend, device_id_type=MESH)
    zero = jnp.zeros((tile, tile), F32)
    for s in range(3):
        sums_user[s, slots] = zero
        sums_item[s, slots] = zero
    for load in small_loads:
        load.wait()
    picks = (user_tiles, item_tiles)
    for s in range(3):

        def link(k, seen, s=s):
            kept = []
            for side in range(2):
                mine = seen[side * tiles : (side + 1) * tiles]
                pick = picks[side][s, 0, k]
                before = slots
                for t in range(tiles):
                    before = jnp.where(pick == t, mine[t], before)
                    kept.append(jnp.where(pick == t, k, mine[t]))
                prev[s, side, k] = before
            return tuple(kept)

        seen = lax.fori_loop(0, slots, link, (jnp.int32(slots),) * (2 * tiles))
        for side in range(2):
            for t in range(tiles):
                last[s, side, t] = seen[side * tiles + t]
    pl.semaphore_wait(barrier, len(friends))

    def remote(src, dst, sems, i, target):
        return pltpu.make_async_remote_copy(
            src_ref=src,
            dst_ref=dst,
            send_sem=sems.at[0, i],
            recv_sem=sems.at[1, i],
            device_id=target,
            device_id_type=MESH,
        )

    def part(h):
        return pl.ds((2 * c + h) * quarter, quarter)

    def far_copy(h):
        return remote(items_hbm.at[part(h)], block_2.at[part(h)], fetch_sem, h, (col(-2), r))

    def near_copy(h, src):
        return remote(src, block_1.at[part(h)], fetch_sem, 2 + h, other if h else same)

    def swap_copy(s, h):
        view = blocks[s].at[part(h)]
        return remote(view, view, swap_sem, 2 * (s - 1) + h, partner)

    for h in range(2):
        far_copy(h).start()

    @pl.when(yl == 1)
    def _():
        for h in range(2):
            near_copy(h, items_hbm.at[part(h)]).start()

    def compute(s):
        for t in range(tiles):
            flipped[t] = blocks[s][t].T
        count = counts[0, 0, s]

        def body(i, carry):
            base = i * GROUP
            held = []
            for g in range(GROUP):
                k = base + g
                u = users[user_tiles[s, 0, k]]
                it = item_tiles[s, 0, k]
                v = blocks[s][it]
                p = jnp.dot(u, flipped[it], preferred_element_type=F32)
                rating = rbuf[s, k].astype(F32)
                live = (k < count).astype(F32)
                e = ((1.0 + CONFIDENCE * rating) * (rating - p) * live).astype(BF16)
                held.append((k, u, v, e))
            for k, u, v, e in held:
                gu = jnp.dot(e, v, preferred_element_type=F32)
                gi = lax.dot_general(e, u, (((0,), (0,)), ((), ())), preferred_element_type=F32)
                sums_user[s, k] = gu + sums_user[s, prev[s, 0, k]]
                sums_item[s, k] = gi + sums_item[s, prev[s, 1, k]]
            return carry

        lax.fori_loop(0, slots // GROUP, body, 0)

    def half_copy(s):
        return remote(half_out.at[s], half_in.at[s], half_sem, s, partner)

    def send_half(s):
        for t in range(tiles):
            end = last[s, 1, t]
            rows = pl.ds(pl.multiple_of((1 - c) * half, half), half)
            half_out[s, t] = sums_item[s, end, rows].astype(BF16)
        half_copy(s).start()

    def piece_copy(s, e):
        return remote(
            chip_sum.at[s, pl.ds(target(e) * per, per)],
            pieces.at[s, e],
            piece_sem,
            s * nq + e,
            (col(1) if s == 1 else b, 2 * target(e) + c),
        )

    def outgoing(s):
        return by_distance + [0] if s == 1 else by_distance

    def send_pieces(s):
        half_copy(s).wait_recv()
        for t in range(tiles):
            end = last[s, 1, t]
            rows = pl.ds(pl.multiple_of(c * half, half), half)
            both = sums_item[s, end, rows] + half_in[s, t].astype(F32)
            chip_sum[s, t] = both.astype(BF16)
        for e in outgoing(s):
            piece_copy(s, e).start()

    def column_sum(s):
        for e in outgoing(s):
            piece_copy(s, e).wait_recv()
        total = None if s == 1 else chip_sum[s, pl.ds(q * per, per)].astype(F32)
        for e in outgoing(s):
            term = pieces[s, e].astype(F32)
            total = term if total is None else total + term
        return total

    def fwd_copy(s):
        return remote(fwd_out, fwd_in, fwd_sem, 0, (col(s), r))

    user_load.wait()
    item_load.wait()
    rating_load(0).wait()
    compute(0)
    send_half(0)

    for h in range(2):
        far_copy(h).wait_recv()
        swap_copy(2, h).start()

        @pl.when(yl == 0)
        def _():
            near_copy(h, block_2.at[part(h)]).start()

    send_pieces(0)
    for h in range(2):
        swap_copy(2, h).wait_recv()
    rating_load(2).wait()
    compute(2)
    send_half(2)

    for h in range(2):
        near_copy(h, items_hbm.at[part(h)]).wait_recv()
        swap_copy(1, h).start()
    send_pieces(2)
    for h in range(2):
        swap_copy(1, h).wait_recv()
    rating_load(1).wait()
    compute(1)
    send_half(1)

    for t in range(tiles):
        grad = zero
        for s in ORDER:
            grad = grad + sums_user[s, last[s, 0, t]]
        old = users[t].astype(F32)
        unew[t] = (old - rate_user * (grad + SHRINKAGE * old)).astype(BF16)
    user_store = pltpu.make_async_copy(unew, user_out, out_sem.at[0])
    user_store.start()

    send_pieces(1)
    fwd_out[...] = column_sum(2)
    fwd_copy(2).start()
    total = column_sum(0)
    fwd_copy(2).wait_recv()
    total = total + fwd_in[...]
    total = total + column_sum(1)

    mine = pl.ds(q * per, per)
    old = block_0[mine, pl.ds(pl.multiple_of(c * half, half), half)].astype(F32)
    inew[mine, c] = (old - rate_item * (total + SHRINKAGE * old)).astype(BF16)

    farthest = [e for e in range(1, nq) if nx > 1 and e // 2 == nx // 2]
    nearer = [e for e in reversed(by_distance) if e not in farthest]

    def gather_copy(e, cross=0):
        view = inew.at[mine, c]
        core = 1 - c if cross else c
        return remote(view, view, gather_sem, cross * nq + e, (b, 2 * target(e) + core))

    def gathered(e, cross=0):
        core = 1 - c if cross else c
        view = inew.at[pl.ds(source(e) * per, per), core]
        return remote(view, view, gather_sem, cross * nq + e, (b, 2 * target(e) + core))

    def pair_copy(e):
        view = inew.at[pl.ds(source(e) * per, per), c]
        return remote(view, view, pair_sem, e, partner)

    def paired(e):
        view = inew.at[pl.ds(source(e) * per, per), 1 - c]
        return remote(view, view, pair_sem, e, partner)

    for e in farthest:
        gather_copy(e).start()
        gather_copy(e, 1).start()
    for e in reversed(nearer):
        gather_copy(e).start()
    pair_copy(0).start()
    for e in nearer:
        gathered(e).wait_recv()
        pair_copy(e).start()
    for e in [0] + nearer:
        paired(e).wait_recv()
    for e in farthest:
        gathered(e).wait_recv()
        gathered(e, 1).wait_recv()
    item_store = pltpu.make_async_copy(inew, item_out, out_sem.at[1])
    item_store.start()

    for h in range(2):
        far_copy(h).wait_send()
        near_copy(h, items_hbm.at[part(h)]).wait_send()
        for s in (1, 2):
            swap_copy(s, h).wait_send()
    for s in ORDER:
        half_copy(s).wait_send()
        for e in outgoing(s):
            piece_copy(s, e).wait_send()
    fwd_copy(2).wait_send()
    for e in farthest:
        gather_copy(e).wait_send()
        gather_copy(e, 1).wait_send()
    for e in nearer:
        gather_copy(e).wait_send()
    for e in [0] + nearer:
        pair_copy(e).wait_send()
    user_store.wait()
    item_store.wait()


def finish(user_raw, item_raw, user_out, item_out, user_buf, item_buf, sem):
    moves = []
    for a, (src, buf, dst) in enumerate(
        ((user_raw, user_buf, user_out), (item_raw, item_buf, item_out))
    ):
        for p in range(2):
            rows = pl.ds(p * (buf.shape[0] // 2), buf.shape[0] // 2)
            i = 2 * a + p
            into = pltpu.make_async_copy(src.at[rows], buf.at[rows], sem.at[0, i])
            away = pltpu.make_async_copy(buf.at[rows], dst.at[rows], sem.at[1, i])
            into.start()
            moves.append((into, away))
    for into, away in moves:
        into.wait()
        away.start()
    for _, away in moves:
        away.wait()


def on_device(users, items, ratings, user_tiles, item_tiles, counts):
    tile = ratings.shape[-1]
    rank = users.shape[1]
    stops, slots = ratings.shape[2:4]
    tiles = users.shape[0] // tile
    half = tile // 2
    nq = lax.axis_size("rep") // 2
    per = tiles // nq
    rate_user = STEP_GAIN / math.sqrt(stops * slots * tile * tile / users.shape[0])
    rate_item = STEP_GAIN / math.sqrt(2 * nq * stops * slots * tile * tile / items.shape[0])
    hbm = pl.BlockSpec(memory_space=pltpu.HBM)
    anywhere = pl.BlockSpec(memory_space=pl.ANY)
    dma = pltpu.SemaphoreType.DMA
    user_new, item_new = pl.pallas_call(
        functools.partial(kernel, rate_user, rate_item),
        out_shape=(
            jax.ShapeDtypeStruct((tiles, tile, rank), BF16),
            jax.ShapeDtypeStruct((tiles, 2, half, rank), BF16),
        ),
        in_specs=[hbm] * 6,
        out_specs=(anywhere, anywhere),
        scratch_shapes=[
            pltpu.VMEM((tiles, tile, rank), BF16),
            pltpu.VMEM((tiles, tile, rank), BF16),
            pltpu.VMEM((tiles, tile, rank), BF16),
            pltpu.VMEM((tiles, tile, rank), BF16),
            pltpu.VMEM((tiles, rank, tile), BF16),
            pltpu.VMEM((stops, slots, tile, tile), BF16),
            pltpu.VMEM((stops, slots + 1, tile, rank), F32),
            pltpu.VMEM((stops, slots + 1, tile, rank), F32),
            pltpu.VMEM((stops, tiles, half, rank), BF16),
            pltpu.VMEM((stops, tiles, half, rank), BF16),
            pltpu.VMEM((stops, tiles, half, rank), BF16),
            pltpu.VMEM((stops, nq, per, half, rank), BF16),
            pltpu.VMEM((per, half, rank), F32),
            pltpu.VMEM((per, half, rank), F32),
            pltpu.VMEM((tiles, tile, rank), BF16),
            pltpu.VMEM((tiles, 2, half, rank), BF16),
            pltpu.SMEM((stops, 1, slots), jnp.int32),
            pltpu.SMEM((stops, 1, slots), jnp.int32),
            pltpu.SMEM((1, 1, stops), jnp.int32),
            pltpu.SMEM((stops, 2, slots), jnp.int32),
            pltpu.SMEM((stops, 2, tiles), jnp.int32),
            dma((8,)),
            dma((2, 4)),
            dma((2, 4)),
            dma((2, 3)),
            dma((2, 3 * nq)),
            dma((2, 1)),
            dma((2, 2 * nq)),
            dma((2, nq)),
            dma((2,)),
        ],
        compiler_params=pltpu.CompilerParams(
            collective_id=0, has_side_effects=True, vmem_limit_bytes=67043328
        ),
    )(
        user_tiles.reshape(stops, 1, slots),
        item_tiles.reshape(stops, 1, slots),
        counts,
        users.reshape(tiles, tile, rank),
        items.reshape(tiles, tile, rank),
        ratings[0, 0],
    )
    user_new = user_new.reshape(users.shape)
    item_new = item_new.reshape(items.shape)
    return pl.pallas_call(
        finish,
        out_shape=(
            jax.ShapeDtypeStruct(users.shape, BF16),
            jax.ShapeDtypeStruct(items.shape, BF16),
        ),
        in_specs=[anywhere, anywhere],
        out_specs=(anywhere, anywhere),
        scratch_shapes=[pltpu.VMEM(users.shape, BF16), pltpu.VMEM(items.shape, BF16), dma((2, 4))],
    )(user_new, item_new)


def solution(mesh):
    return jax.shard_map(
        on_device,
        mesh=mesh,
        in_specs=(
            P(("blk", "rep"), None),
            P("blk", None),
            P("blk", "rep", None, None, None, None),
            P("blk", "rep", None, None),
            P("blk", "rep", None, None),
            P("blk", "rep", None),
        ),
        out_specs=(P(("blk", "rep"), None), P("blk", None)),
        check_vma=False,
    )
```

```python
import functools
import math

import jax
import jax.numpy as jnp
from jax import lax
from jax.experimental import pallas as pl
from jax.experimental.pallas import tpu as pltpu
from jax.sharding import PartitionSpec as P

CONFIDENCE = 0.5
SHRINKAGE = 0.05
STEP_GAIN = 0.3
GROUP = 20
MESH = pl.DeviceIdType.MESH
F32 = jnp.float32
BF16 = jnp.bfloat16
ORDER = (0, 2, 1)


def kernel(
    rate_user,
    rate_item,
    user_tiles_hbm,
    item_tiles_hbm,
    counts_hbm,
    users_hbm,
    items_hbm,
    ratings_hbm,
    user_out,
    item_out,
    users,
    block_0,
    block_1,
    block_2,
    flipped,
    rbuf,
    sums_user,
    sums_item,
    half_out,
    half_in,
    chip_sum,
    pieces,
    fwd_out,
    fwd_in,
    unew,
    inew,
    user_tiles,
    item_tiles,
    counts,
    tile_rows,
    picks,
    links,
    table,
    load_sem,
    fetch_sem,
    swap_sem,
    half_sem,
    piece_sem,
    fwd_sem,
    gather_sem,
    pair_sem,
    out_sem,
):
    blocks = (block_0, block_1, block_2)
    nblk = lax.axis_size("blk")
    nrep = lax.axis_size("rep")
    nq = nrep // 2
    tiles, tile, _ = users.shape
    slots = rbuf.shape[1]
    half = tile // 2
    per = tiles // nq
    quarter = tiles // 4
    b = lax.axis_index("blk")
    r = lax.axis_index("rep")
    yl = b % 2
    q = r // 2
    c = r % 2
    yh = q % 2
    x = q // 2
    nx = nq // 2

    def col(distance):
        return (b + nblk + distance) % nblk

    def target(e):
        return 2 * ((x + e // 2) % nx) + (yh + e) % 2

    def source(e):
        return 2 * ((x + nx - e // 2) % nx) + (yh + e) % 2

    by_distance = sorted(range(1, nq), key=lambda e: (-min(e // 2, nx - e // 2), -(e % 2)))
    partner = (b, r + 1 - 2 * c)
    near = b + 1 - 2 * yl
    same = (near, r)
    other = (near, r + 2 - 4 * yh)

    def rating_load(s):
        return pltpu.make_async_copy(ratings_hbm.at[s], rbuf.at[s], load_sem.at[s])

    user_load = pltpu.make_async_copy(users_hbm, users, load_sem.at[3])
    item_load = pltpu.make_async_copy(items_hbm, block_0, load_sem.at[4])
    small = [
        (user_tiles_hbm, tile_rows.at[0]),
        (item_tiles_hbm, tile_rows.at[1]),
        (user_tiles_hbm, user_tiles),
        (item_tiles_hbm, item_tiles),
        (counts_hbm, counts),
    ]
    small_loads = [
        pltpu.make_async_copy(src, dst, load_sem.at[5 + i]) for i, (src, dst) in enumerate(small)
    ]
    for load in small_loads:
        load.start()
    user_load.start()
    item_load.start()
    for s in ORDER:
        rating_load(s).start()

    barrier = pltpu.get_barrier_semaphore()
    friends = [partner, (col(-2), r), (col(2), r)]
    friends += [(col(s), 2 * target(e) + c) for s in (1, -1) for e in range(nq)]
    friends += [(b, 2 * target(e) + c) for e in range(1, nq)]
    friends += [(b, 2 * target(e) + 1 - c) for e in range(1, nq) if nx > 1 and e // 2 == nx // 2]
    for friend in friends:
        pl.semaphore_signal(barrier, inc=1, device_id=friend, device_id_type=MESH)
    zero = jnp.zeros((tile, tile), F32)
    pl.semaphore_wait(barrier, len(friends))

    def remote(src, dst, sems, i, target):
        return pltpu.make_async_remote_copy(
            src_ref=src,
            dst_ref=dst,
            send_sem=sems.at[0, i],
            recv_sem=sems.at[1, i],
            device_id=target,
            device_id_type=MESH,
        )

    def part(h):
        return pl.ds((2 * c + h) * quarter, quarter)

    def far_copy(h):
        return remote(items_hbm.at[part(h)], block_2.at[part(h)], fetch_sem, h, (col(-2), r))

    def near_copy(h, src):
        return remote(src, block_1.at[part(h)], fetch_sem, 2 + h, other if h else same)

    def swap_copy(s, h):
        view = blocks[s].at[part(h)]
        return remote(view, view, swap_sem, 2 * (s - 1) + h, partner)

    for h in range(2):
        far_copy(h).start()

    @pl.when(yl == 1)
    def _():
        for h in range(2):
            near_copy(h, items_hbm.at[part(h)]).start()

    for load in small_loads[:2]:
        load.wait()
    lane = lax.broadcasted_iota(jnp.int32, picks.shape, 1)
    picks[...] = lane - slots
    for side in range(2):
        for s in range(3):
            picks[pl.ds(3 * side + s, 1), pl.ds(0, slots)] = tile_rows[side, s]
    wanted = picks[...]
    found = jnp.full_like(wanted, slots)
    for k in range(slots):
        hit = (wanted == jnp.broadcast_to(wanted[:, k : k + 1], wanted.shape)) & (lane > k)
        found = jnp.where(hit, k, found)
    links[...] = found
    table_copy = pltpu.make_async_copy(links, table, load_sem.at[10])
    table_copy.start()
    for s in range(3):
        sums_user[s, slots] = zero
        sums_item[s, slots] = zero
    for load in small_loads[2:]:
        load.wait()
    table_copy.wait()

    def compute(s):
        for t in range(tiles):
            flipped[t] = blocks[s][t].T
        count = counts[0, 0, s]

        def body(i, carry):
            base = i * GROUP
            held = []
            for g in range(GROUP):
                k = base + g
                u = users[user_tiles[s, 0, k]]
                it = item_tiles[s, 0, k]
                v = blocks[s][it]
                p = jnp.dot(u, flipped[it], preferred_element_type=F32)
                rating = rbuf[s, k].astype(F32)
                live = (k < count).astype(F32)
                e = ((1.0 + CONFIDENCE * rating) * (rating - p) * live).astype(BF16)
                held.append((k, u, v, e))
            for k, u, v, e in held:
                gu = jnp.dot(e, v, preferred_element_type=F32)
                gi = lax.dot_general(e, u, (((0,), (0,)), ((), ())), preferred_element_type=F32)
                sums_user[s, k] = gu + sums_user[s, table[s, k]]
                sums_item[s, k] = gi + sums_item[s, table[3 + s, k]]
            return carry

        lax.fori_loop(0, slots // GROUP, body, 0)

    def half_copy(s):
        return remote(half_out.at[s], half_in.at[s], half_sem, s, partner)

    def send_half(s):
        for t in range(tiles):
            end = table[3 + s, slots + t]
            rows = pl.ds(pl.multiple_of((1 - c) * half, half), half)
            half_out[s, t] = sums_item[s, end, rows].astype(BF16)
        half_copy(s).start()

    def piece_copy(s, e):
        return remote(
            chip_sum.at[s, pl.ds(target(e) * per, per)],
            pieces.at[s, e],
            piece_sem,
            s * nq + e,
            (col(1) if s == 1 else b, 2 * target(e) + c),
        )

    def outgoing(s):
        return by_distance + [0] if s == 1 else by_distance

    def send_pieces(s):
        half_copy(s).wait_recv()
        for t in range(tiles):
            end = table[3 + s, slots + t]
            rows = pl.ds(pl.multiple_of(c * half, half), half)
            both = sums_item[s, end, rows] + half_in[s, t].astype(F32)
            chip_sum[s, t] = both.astype(BF16)
        for e in outgoing(s):
            piece_copy(s, e).start()

    def column_sum(s):
        for e in outgoing(s):
            piece_copy(s, e).wait_recv()
        total = None if s == 1 else chip_sum[s, pl.ds(q * per, per)].astype(F32)
        for e in outgoing(s):
            term = pieces[s, e].astype(F32)
            total = term if total is None else total + term
        return total

    def fwd_copy(s):
        return remote(fwd_out, fwd_in, fwd_sem, 0, (col(s), r))

    user_load.wait()
    item_load.wait()
    rating_load(0).wait()
    compute(0)
    send_half(0)

    for h in range(2):
        far_copy(h).wait_recv()
        swap_copy(2, h).start()

        @pl.when(yl == 0)
        def _():
            near_copy(h, block_2.at[part(h)]).start()

    send_pieces(0)
    for h in range(2):
        swap_copy(2, h).wait_recv()
    rating_load(2).wait()
    compute(2)
    send_half(2)

    for h in range(2):
        near_copy(h, items_hbm.at[part(h)]).wait_recv()
        swap_copy(1, h).start()
    send_pieces(2)
    for h in range(2):
        swap_copy(1, h).wait_recv()
    rating_load(1).wait()
    compute(1)
    send_half(1)

    for t in range(tiles):
        grad = zero
        for s in ORDER:
            grad = grad + sums_user[s, table[s, slots + t]]
        old = users[t].astype(F32)
        unew[t] = (old - rate_user * (grad + SHRINKAGE * old)).astype(BF16)
    user_store = pltpu.make_async_copy(unew, user_out, out_sem.at[0])
    user_store.start()

    send_pieces(1)
    fwd_out[...] = column_sum(2)
    fwd_copy(2).start()
    total = column_sum(0)
    fwd_copy(2).wait_recv()
    total = total + fwd_in[...]
    total = total + column_sum(1)

    mine = pl.ds(q * per, per)
    old = block_0[mine, pl.ds(pl.multiple_of(c * half, half), half)].astype(F32)
    inew[mine, c] = (old - rate_item * (total + SHRINKAGE * old)).astype(BF16)

    farthest = [e for e in range(1, nq) if nx > 1 and e // 2 == nx // 2]
    nearer = [e for e in reversed(by_distance) if e not in farthest]

    def gather_copy(e, cross=0):
        view = inew.at[mine, c]
        core = 1 - c if cross else c
        return remote(view, view, gather_sem, cross * nq + e, (b, 2 * target(e) + core))

    def gathered(e, cross=0):
        core = 1 - c if cross else c
        view = inew.at[pl.ds(source(e) * per, per), core]
        return remote(view, view, gather_sem, cross * nq + e, (b, 2 * target(e) + core))

    def pair_copy(e):
        view = inew.at[pl.ds(source(e) * per, per), c]
        return remote(view, view, pair_sem, e, partner)

    def paired(e):
        view = inew.at[pl.ds(source(e) * per, per), 1 - c]
        return remote(view, view, pair_sem, e, partner)

    for e in farthest:
        gather_copy(e).start()
        gather_copy(e, 1).start()
    for e in reversed(nearer):
        gather_copy(e).start()
    pair_copy(0).start()
    for e in nearer:
        gathered(e).wait_recv()
        pair_copy(e).start()
    for e in [0] + nearer:
        paired(e).wait_recv()
    for e in farthest:
        gathered(e).wait_recv()
        gathered(e, 1).wait_recv()
    item_store = pltpu.make_async_copy(inew, item_out, out_sem.at[1])
    item_store.start()

    for h in range(2):
        far_copy(h).wait_send()
        near_copy(h, items_hbm.at[part(h)]).wait_send()
        for s in (1, 2):
            swap_copy(s, h).wait_send()
    for s in ORDER:
        half_copy(s).wait_send()
        for e in outgoing(s):
            piece_copy(s, e).wait_send()
    fwd_copy(2).wait_send()
    for e in farthest:
        gather_copy(e).wait_send()
        gather_copy(e, 1).wait_send()
    for e in nearer:
        gather_copy(e).wait_send()
    for e in [0] + nearer:
        pair_copy(e).wait_send()
    user_store.wait()
    item_store.wait()


def finish(user_raw, item_raw, user_out, item_out, user_buf, item_buf, sem):
    moves = []
    for a, (src, buf, dst) in enumerate(
        ((user_raw, user_buf, user_out), (item_raw, item_buf, item_out))
    ):
        for p in range(2):
            rows = pl.ds(p * (buf.shape[0] // 2), buf.shape[0] // 2)
            i = 2 * a + p
            into = pltpu.make_async_copy(src.at[rows], buf.at[rows], sem.at[0, i])
            away = pltpu.make_async_copy(buf.at[rows], dst.at[rows], sem.at[1, i])
            into.start()
            moves.append((into, away))
    for into, away in moves:
        into.wait()
        away.start()
    for _, away in moves:
        away.wait()


def on_device(users, items, ratings, user_tiles, item_tiles, counts):
    tile = ratings.shape[-1]
    rank = users.shape[1]
    stops, slots = ratings.shape[2:4]
    tiles = users.shape[0] // tile
    half = tile // 2
    nq = lax.axis_size("rep") // 2
    per = tiles // nq
    rate_user = STEP_GAIN / math.sqrt(stops * slots * tile * tile / users.shape[0])
    rate_item = STEP_GAIN / math.sqrt(2 * nq * stops * slots * tile * tile / items.shape[0])
    hbm = pl.BlockSpec(memory_space=pltpu.HBM)
    anywhere = pl.BlockSpec(memory_space=pl.ANY)
    dma = pltpu.SemaphoreType.DMA
    user_new, item_new = pl.pallas_call(
        functools.partial(kernel, rate_user, rate_item),
        out_shape=(
            jax.ShapeDtypeStruct((tiles, tile, rank), BF16),
            jax.ShapeDtypeStruct((tiles, 2, half, rank), BF16),
        ),
        in_specs=[hbm] * 6,
        out_specs=(anywhere, anywhere),
        scratch_shapes=[
            pltpu.VMEM((tiles, tile, rank), BF16),
            pltpu.VMEM((tiles, tile, rank), BF16),
            pltpu.VMEM((tiles, tile, rank), BF16),
            pltpu.VMEM((tiles, tile, rank), BF16),
            pltpu.VMEM((tiles, rank, tile), BF16),
            pltpu.VMEM((stops, slots, tile, tile), BF16),
            pltpu.VMEM((stops, slots + 1, tile, rank), F32),
            pltpu.VMEM((stops, slots + 1, tile, rank), F32),
            pltpu.VMEM((stops, tiles, half, rank), BF16),
            pltpu.VMEM((stops, tiles, half, rank), BF16),
            pltpu.VMEM((stops, tiles, half, rank), BF16),
            pltpu.VMEM((stops, nq, per, half, rank), BF16),
            pltpu.VMEM((per, half, rank), F32),
            pltpu.VMEM((per, half, rank), F32),
            pltpu.VMEM((tiles, tile, rank), BF16),
            pltpu.VMEM((tiles, 2, half, rank), BF16),
            pltpu.SMEM((stops, 1, slots), jnp.int32),
            pltpu.SMEM((stops, 1, slots), jnp.int32),
            pltpu.SMEM((1, 1, stops), jnp.int32),
            pltpu.VMEM((2, stops, 1, slots), jnp.int32),
            pltpu.VMEM((8, 128), jnp.int32),
            pltpu.VMEM((8, 128), jnp.int32),
            pltpu.SMEM((8, 128), jnp.int32),
            dma((11,)),
            dma((2, 4)),
            dma((2, 4)),
            dma((2, 3)),
            dma((2, 3 * nq)),
            dma((2, 1)),
            dma((2, 2 * nq)),
            dma((2, nq)),
            dma((2,)),
        ],
        compiler_params=pltpu.CompilerParams(
            collective_id=0, has_side_effects=True, vmem_limit_bytes=67043328
        ),
    )(
        user_tiles.reshape(stops, 1, slots),
        item_tiles.reshape(stops, 1, slots),
        counts,
        users.reshape(tiles, tile, rank),
        items.reshape(tiles, tile, rank),
        ratings[0, 0],
    )
    user_new = user_new.reshape(users.shape)
    item_new = item_new.reshape(items.shape)
    return pl.pallas_call(
        finish,
        out_shape=(
            jax.ShapeDtypeStruct(users.shape, BF16),
            jax.ShapeDtypeStruct(items.shape, BF16),
        ),
        in_specs=[anywhere, anywhere],
        out_specs=(anywhere, anywhere),
        scratch_shapes=[pltpu.VMEM(users.shape, BF16), pltpu.VMEM(items.shape, BF16), dma((2, 4))],
    )(user_new, item_new)


def solution(mesh):
    return jax.shard_map(
        on_device,
        mesh=mesh,
        in_specs=(
            P(("blk", "rep"), None),
            P("blk", None),
            P("blk", "rep", None, None, None, None),
            P("blk", "rep", None, None),
            P("blk", "rep", None, None),
            P("blk", "rep", None),
        ),
        out_specs=(P(("blk", "rep"), None), P("blk", None)),
        check_vma=False,
    )
```

```python
import functools
import math

import jax
import jax.numpy as jnp
from jax import lax
from jax.experimental import pallas as pl
from jax.experimental.pallas import tpu as pltpu
from jax.sharding import PartitionSpec as P

CONFIDENCE = 0.5
SHRINKAGE = 0.05
STEP_GAIN = 0.3
GROUP = 20
MESH = pl.DeviceIdType.MESH
F32 = jnp.float32
BF16 = jnp.bfloat16
ORDER = (0, 2, 1)


def kernel(
    rate_user,
    rate_item,
    user_tiles_hbm,
    item_tiles_hbm,
    counts_hbm,
    users_hbm,
    items_hbm,
    ratings_hbm,
    user_out,
    item_out,
    users,
    block_0,
    block_1,
    block_2,
    flipped,
    rbuf,
    sums_user,
    sums_item,
    half_out,
    half_in,
    chip_sum,
    pieces,
    fwd_out,
    fwd_in,
    unew,
    inew,
    user_tiles,
    item_tiles,
    counts,
    tile_rows,
    picks,
    links,
    table,
    load_sem,
    fetch_sem,
    swap_sem,
    half_sem,
    piece_sem,
    fwd_sem,
    gather_sem,
    out_sem,
):
    blocks = (block_0, block_1, block_2)
    nblk = lax.axis_size("blk")
    nrep = lax.axis_size("rep")
    nq = nrep // 2
    tiles, tile, _ = users.shape
    slots = rbuf.shape[1]
    half = tile // 2
    per = tiles // nq
    quarter = tiles // 4
    b = lax.axis_index("blk")
    r = lax.axis_index("rep")
    yl = b % 2
    q = r // 2
    c = r % 2
    yh = q % 2
    x = q // 2
    nx = nq // 2

    def col(distance):
        return (b + nblk + distance) % nblk

    def target(e):
        return 2 * ((x + e // 2) % nx) + (yh + e) % 2

    def source(e):
        return 2 * ((x + nx - e // 2) % nx) + (yh + e) % 2

    by_distance = sorted(range(1, nq), key=lambda e: (-min(e // 2, nx - e // 2), -(e % 2)))
    partner = (b, r + 1 - 2 * c)
    near = b + 1 - 2 * yl
    same = (near, r)
    other = (near, r + 2 - 4 * yh)

    def rating_load(s):
        return pltpu.make_async_copy(ratings_hbm.at[s], rbuf.at[s], load_sem.at[s])

    user_load = pltpu.make_async_copy(users_hbm, users, load_sem.at[3])
    item_load = pltpu.make_async_copy(items_hbm, block_0, load_sem.at[4])
    small = [
        (user_tiles_hbm, tile_rows.at[0]),
        (item_tiles_hbm, tile_rows.at[1]),
        (user_tiles_hbm, user_tiles),
        (item_tiles_hbm, item_tiles),
        (counts_hbm, counts),
    ]
    small_loads = [
        pltpu.make_async_copy(src, dst, load_sem.at[5 + i]) for i, (src, dst) in enumerate(small)
    ]
    for load in small_loads:
        load.start()
    user_load.start()
    item_load.start()
    for s in ORDER:
        rating_load(s).start()

    barrier = pltpu.get_barrier_semaphore()
    friends = [partner, (col(-2), r), (col(2), r)]
    friends += [(col(s), 2 * target(e) + c) for s in (1, -1) for e in range(nq)]
    friends += [(b, 2 * target(e) + c) for e in range(1, nq)]
    friends += [(b, 2 * target(e) + 1 - c) for e in range(1, nq)]
    for friend in friends:
        pl.semaphore_signal(barrier, inc=1, device_id=friend, device_id_type=MESH)
    zero = jnp.zeros((tile, tile), F32)
    pl.semaphore_wait(barrier, len(friends))

    def remote(src, dst, sems, i, target):
        return pltpu.make_async_remote_copy(
            src_ref=src,
            dst_ref=dst,
            send_sem=sems.at[0, i],
            recv_sem=sems.at[1, i],
            device_id=target,
            device_id_type=MESH,
        )

    def part(h):
        return pl.ds((2 * c + h) * quarter, quarter)

    def far_copy(h):
        return remote(items_hbm.at[part(h)], block_2.at[part(h)], fetch_sem, h, (col(-2), r))

    def near_copy(h, src):
        return remote(src, block_1.at[part(h)], fetch_sem, 2 + h, other if h else same)

    def swap_copy(s, h):
        view = blocks[s].at[part(h)]
        return remote(view, view, swap_sem, 2 * (s - 1) + h, partner)

    for h in range(2):
        far_copy(h).start()

    @pl.when(yl == 1)
    def _():
        for h in range(2):
            near_copy(h, items_hbm.at[part(h)]).start()

    for load in small_loads[:2]:
        load.wait()
    lane = lax.broadcasted_iota(jnp.int32, picks.shape, 1)
    picks[...] = lane - slots
    for side in range(2):
        for s in range(3):
            picks[pl.ds(3 * side + s, 1), pl.ds(0, slots)] = tile_rows[side, s]
    wanted = picks[...]
    found = jnp.full_like(wanted, slots)
    for k in range(slots):
        hit = (wanted == jnp.broadcast_to(wanted[:, k : k + 1], wanted.shape)) & (lane > k)
        found = jnp.where(hit, k, found)
    links[...] = found
    table_copy = pltpu.make_async_copy(links, table, load_sem.at[10])
    table_copy.start()
    for s in range(3):
        sums_user[s, slots] = zero
        sums_item[s, slots] = zero
    for load in small_loads[2:]:
        load.wait()
    table_copy.wait()

    def compute(s):
        for t in range(tiles):
            flipped[t] = blocks[s][t].T
        count = counts[0, 0, s]

        def body(i, carry):
            base = i * GROUP
            held = []
            for g in range(GROUP):
                k = base + g
                u = users[user_tiles[s, 0, k]]
                it = item_tiles[s, 0, k]
                v = blocks[s][it]
                p = jnp.dot(u, flipped[it], preferred_element_type=F32)
                rating = rbuf[s, k].astype(F32)
                live = (k < count).astype(F32)
                e = ((1.0 + CONFIDENCE * rating) * (rating - p) * live).astype(BF16)
                held.append((k, u, v, e))
            for k, u, v, e in held:
                gu = jnp.dot(e, v, preferred_element_type=F32)
                gi = lax.dot_general(e, u, (((0,), (0,)), ((), ())), preferred_element_type=F32)
                sums_user[s, k] = gu + sums_user[s, table[s, k]]
                sums_item[s, k] = gi + sums_item[s, table[3 + s, k]]
            return carry

        lax.fori_loop(0, slots // GROUP, body, 0)

    def half_copy(s):
        return remote(half_out.at[s], half_in.at[s], half_sem, s, partner)

    def send_half(s):
        for t in range(tiles):
            end = table[3 + s, slots + t]
            rows = pl.ds(pl.multiple_of((1 - c) * half, half), half)
            half_out[s, t] = sums_item[s, end, rows].astype(BF16)
        half_copy(s).start()

    def piece_copy(s, e):
        return remote(
            chip_sum.at[s, pl.ds(target(e) * per, per)],
            pieces.at[s, e],
            piece_sem,
            s * nq + e,
            (col(1) if s == 1 else b, 2 * target(e) + c),
        )

    def outgoing(s):
        return by_distance + [0] if s == 1 else by_distance

    def send_pieces(s):
        half_copy(s).wait_recv()
        for t in range(tiles):
            end = table[3 + s, slots + t]
            rows = pl.ds(pl.multiple_of(c * half, half), half)
            both = sums_item[s, end, rows] + half_in[s, t].astype(F32)
            chip_sum[s, t] = both.astype(BF16)
        for e in outgoing(s):
            piece_copy(s, e).start()

    def column_sum(s):
        for e in outgoing(s):
            piece_copy(s, e).wait_recv()
        total = None if s == 1 else chip_sum[s, pl.ds(q * per, per)].astype(F32)
        for e in outgoing(s):
            term = pieces[s, e].astype(F32)
            total = term if total is None else total + term
        return total

    def fwd_copy(s):
        return remote(fwd_out, fwd_in, fwd_sem, 0, (col(s), r))

    user_load.wait()
    item_load.wait()
    rating_load(0).wait()
    compute(0)
    send_half(0)

    for h in range(2):
        far_copy(h).wait_recv()
        swap_copy(2, h).start()

        @pl.when(yl == 0)
        def _():
            near_copy(h, block_2.at[part(h)]).start()

    send_pieces(0)
    for h in range(2):
        swap_copy(2, h).wait_recv()
    rating_load(2).wait()
    compute(2)
    send_half(2)

    for h in range(2):
        near_copy(h, items_hbm.at[part(h)]).wait_recv()
        swap_copy(1, h).start()
    send_pieces(2)
    for h in range(2):
        swap_copy(1, h).wait_recv()
    rating_load(1).wait()
    compute(1)
    send_half(1)

    for t in range(tiles):
        grad = zero
        for s in ORDER:
            grad = grad + sums_user[s, table[s, slots + t]]
        old = users[t].astype(F32)
        unew[t] = (old - rate_user * (grad + SHRINKAGE * old)).astype(BF16)
    user_store = pltpu.make_async_copy(unew, user_out, out_sem.at[0])
    user_store.start()

    send_pieces(1)
    fwd_out[...] = column_sum(2)
    fwd_copy(2).start()
    total = column_sum(0)
    fwd_copy(2).wait_recv()
    total = total + fwd_in[...]
    total = total + column_sum(1)

    mine = pl.ds(q * per, per)
    old = block_0[mine, pl.ds(pl.multiple_of(c * half, half), half)].astype(F32)
    inew[mine, c] = (old - rate_item * (total + SHRINKAGE * old)).astype(BF16)

    def gather_copy(e, cross=0):
        view = inew.at[mine, c]
        core = 1 - c if cross else c
        return remote(view, view, gather_sem, cross * nq + e, (b, 2 * target(e) + core))

    def gathered(e, cross=0):
        core = 1 - c if cross else c
        view = inew.at[pl.ds(source(e) * per, per), core]
        return remote(view, view, gather_sem, cross * nq + e, (b, 2 * target(e) + core))

    gathers = [(e, cross) for e in by_distance for cross in (0, 1)] + [(0, 1)]
    for e, cross in gathers:
        gather_copy(e, cross).start()
    for e, cross in reversed(gathers):
        gathered(e, cross).wait_recv()
    item_store = pltpu.make_async_copy(inew, item_out, out_sem.at[1])
    item_store.start()

    for h in range(2):
        far_copy(h).wait_send()
        near_copy(h, items_hbm.at[part(h)]).wait_send()
        for s in (1, 2):
            swap_copy(s, h).wait_send()
    for s in ORDER:
        half_copy(s).wait_send()
        for e in outgoing(s):
            piece_copy(s, e).wait_send()
    fwd_copy(2).wait_send()
    for e, cross in gathers:
        gather_copy(e, cross).wait_send()
    user_store.wait()
    item_store.wait()


def finish(user_new, item_new, user_out, item_out, sem):
    moves = [
        pltpu.make_async_copy(user_new, user_out, sem.at[0]),
        pltpu.make_async_copy(item_new, item_out, sem.at[1]),
    ]
    for move in moves:
        move.start()
    for move in moves:
        move.wait()


def on_device(users, items, ratings, user_tiles, item_tiles, counts):
    tile = ratings.shape[-1]
    rank = users.shape[1]
    stops, slots = ratings.shape[2:4]
    tiles = users.shape[0] // tile
    half = tile // 2
    nq = lax.axis_size("rep") // 2
    per = tiles // nq
    rate_user = STEP_GAIN / math.sqrt(stops * slots * tile * tile / users.shape[0])
    rate_item = STEP_GAIN / math.sqrt(2 * nq * stops * slots * tile * tile / items.shape[0])
    hbm = pl.BlockSpec(memory_space=pltpu.HBM)
    anywhere = pl.BlockSpec(memory_space=pl.ANY)
    dma = pltpu.SemaphoreType.DMA
    user_new, item_new = pl.pallas_call(
        functools.partial(kernel, rate_user, rate_item),
        out_shape=(
            pltpu.VMEM((tiles, tile, rank), BF16),
            pltpu.VMEM((tiles, 2, half, rank), BF16),
        ),
        in_specs=[hbm] * 6,
        out_specs=(anywhere, anywhere),
        scratch_shapes=[
            pltpu.VMEM((tiles, tile, rank), BF16),
            pltpu.VMEM((tiles, tile, rank), BF16),
            pltpu.VMEM((tiles, tile, rank), BF16),
            pltpu.VMEM((tiles, tile, rank), BF16),
            pltpu.VMEM((tiles, rank, tile), BF16),
            pltpu.VMEM((stops, slots, tile, tile), BF16),
            pltpu.VMEM((stops, slots + 1, tile, rank), F32),
            pltpu.VMEM((stops, slots + 1, tile, rank), F32),
            pltpu.VMEM((stops, tiles, half, rank), BF16),
            pltpu.VMEM((stops, tiles, half, rank), BF16),
            pltpu.VMEM((stops, tiles, half, rank), BF16),
            pltpu.VMEM((stops, nq, per, half, rank), BF16),
            pltpu.VMEM((per, half, rank), F32),
            pltpu.VMEM((per, half, rank), F32),
            pltpu.VMEM((tiles, tile, rank), BF16),
            pltpu.VMEM((tiles, 2, half, rank), BF16),
            pltpu.SMEM((stops, 1, slots), jnp.int32),
            pltpu.SMEM((stops, 1, slots), jnp.int32),
            pltpu.SMEM((1, 1, stops), jnp.int32),
            pltpu.VMEM((2, stops, 1, slots), jnp.int32),
            pltpu.VMEM((8, 128), jnp.int32),
            pltpu.VMEM((8, 128), jnp.int32),
            pltpu.SMEM((8, 128), jnp.int32),
            dma((11,)),
            dma((2, 4)),
            dma((2, 4)),
            dma((2, 3)),
            dma((2, 3 * nq)),
            dma((2, 1)),
            dma((2, 2 * nq)),
            dma((2,)),
        ],
        compiler_params=pltpu.CompilerParams(
            collective_id=0, has_side_effects=True, vmem_limit_bytes=60000000
        ),
    )(
        user_tiles.reshape(stops, 1, slots),
        item_tiles.reshape(stops, 1, slots),
        counts,
        users.reshape(tiles, tile, rank),
        items.reshape(tiles, tile, rank),
        ratings[0, 0],
    )
    user_new = user_new.reshape(users.shape)
    item_new = item_new.reshape(items.shape)
    return pl.pallas_call(
        finish,
        out_shape=(
            jax.ShapeDtypeStruct(users.shape, BF16),
            jax.ShapeDtypeStruct(items.shape, BF16),
        ),
        in_specs=[pl.BlockSpec(memory_space=pltpu.VMEM)] * 2,
        out_specs=(anywhere, anywhere),
        scratch_shapes=[dma((2,))],
        compiler_params=pltpu.CompilerParams(vmem_limit_bytes=4 << 20),
    )(user_new, item_new)


def solution(mesh):
    return jax.shard_map(
        on_device,
        mesh=mesh,
        in_specs=(
            P(("blk", "rep"), None),
            P("blk", None),
            P("blk", "rep", None, None, None, None),
            P("blk", "rep", None, None),
            P("blk", "rep", None, None),
            P("blk", "rep", None),
        ),
        out_specs=(P(("blk", "rep"), None), P("blk", None)),
        check_vma=False,
    )
```

```python
import functools
import math

import jax
import jax.numpy as jnp
from jax import lax
from jax.experimental import pallas as pl
from jax.experimental.pallas import tpu as pltpu
from jax.sharding import PartitionSpec as P

CONFIDENCE = 0.5
SHRINKAGE = 0.05
STEP_GAIN = 0.3
GROUP = 40
MESH = pl.DeviceIdType.MESH
F32 = jnp.float32
BF16 = jnp.bfloat16
ORDER = (0, 2, 1)


def kernel(
    rate_user,
    rate_item,
    user_tiles_hbm,
    item_tiles_hbm,
    counts_hbm,
    users_hbm,
    items_hbm,
    ratings_hbm,
    user_out,
    item_out,
    users,
    block_0,
    block_1,
    block_2,
    flipped,
    rbuf,
    sums_user,
    sums_item,
    half_out,
    half_in,
    chip_sum,
    pieces,
    fwd_out,
    fwd_in,
    unew,
    inew,
    user_tiles,
    item_tiles,
    counts,
    tile_rows,
    picks,
    links,
    table,
    load_sem,
    fetch_sem,
    swap_sem,
    half_sem,
    piece_sem,
    fwd_sem,
    gather_sem,
    out_sem,
):
    blocks = (block_0, block_1, block_2)
    nblk = lax.axis_size("blk")
    nrep = lax.axis_size("rep")
    nq = nrep // 2
    tiles, tile, _ = users.shape
    slots = rbuf.shape[1]
    half = tile // 2
    per = tiles // nq
    quarter = tiles // 4
    b = lax.axis_index("blk")
    r = lax.axis_index("rep")
    yl = b % 2
    q = r // 2
    c = r % 2
    yh = q % 2
    x = q // 2
    nx = nq // 2

    def col(distance):
        return (b + nblk + distance) % nblk

    def target(e):
        return 2 * ((x + e // 2) % nx) + (yh + e) % 2

    def source(e):
        return 2 * ((x + nx - e // 2) % nx) + (yh + e) % 2

    by_distance = sorted(range(1, nq), key=lambda e: (-min(e // 2, nx - e // 2), -(e % 2)))
    partner = (b, r + 1 - 2 * c)
    near = b + 1 - 2 * yl
    same = (near, r)
    other = (near, r + 2 - 4 * yh)

    def rating_load(s):
        return pltpu.make_async_copy(ratings_hbm.at[s], rbuf.at[s], load_sem.at[s])

    user_load = pltpu.make_async_copy(users_hbm, users, load_sem.at[3])
    item_load = pltpu.make_async_copy(items_hbm, block_0, load_sem.at[4])
    small = [
        (user_tiles_hbm, tile_rows.at[0]),
        (item_tiles_hbm, tile_rows.at[1]),
        (user_tiles_hbm, user_tiles),
        (item_tiles_hbm, item_tiles),
        (counts_hbm, counts),
    ]
    small_loads = [
        pltpu.make_async_copy(src, dst, load_sem.at[5 + i]) for i, (src, dst) in enumerate(small)
    ]
    for load in small_loads:
        load.start()
    user_load.start()
    item_load.start()
    for s in ORDER:
        rating_load(s).start()

    barrier = pltpu.get_barrier_semaphore()
    friends = [partner, (col(-2), r), (col(2), r)]
    friends += [(col(s), 2 * target(e) + c) for s in (1, -1) for e in range(nq)]
    friends += [(b, 2 * target(e) + c) for e in range(1, nq)]
    friends += [(b, 2 * target(e) + 1 - c) for e in range(1, nq)]
    for friend in friends:
        pl.semaphore_signal(barrier, inc=1, device_id=friend, device_id_type=MESH)
    zero = jnp.zeros((tile, tile), F32)
    pl.semaphore_wait(barrier, len(friends))

    def remote(src, dst, sems, i, target):
        return pltpu.make_async_remote_copy(
            src_ref=src,
            dst_ref=dst,
            send_sem=sems.at[0, i],
            recv_sem=sems.at[1, i],
            device_id=target,
            device_id_type=MESH,
        )

    def part(h):
        return pl.ds((2 * c + h) * quarter, quarter)

    def far_copy(h):
        return remote(items_hbm.at[part(h)], block_2.at[part(h)], fetch_sem, h, (col(-2), r))

    def near_copy(h, src):
        return remote(src, block_1.at[part(h)], fetch_sem, 2 + h, other if h else same)

    def swap_copy(s, h):
        view = blocks[s].at[part(h)]
        return remote(view, view, swap_sem, 2 * (s - 1) + h, partner)

    for h in range(2):
        far_copy(h).start()

    @pl.when(yl == 1)
    def _():
        for h in range(2):
            near_copy(h, items_hbm.at[part(h)]).start()

    for load in small_loads[:2]:
        load.wait()
    lane = lax.broadcasted_iota(jnp.int32, picks.shape, 1)
    picks[...] = lane - slots
    for side in range(2):
        for s in range(3):
            picks[pl.ds(3 * side + s, 1), pl.ds(0, slots)] = tile_rows[side, s]
    wanted = picks[...]
    found = jnp.full_like(wanted, slots)
    for k in range(slots):
        hit = (wanted == jnp.broadcast_to(wanted[:, k : k + 1], wanted.shape)) & (lane > k)
        found = jnp.where(hit, k, found)
    links[...] = found
    table_copy = pltpu.make_async_copy(links, table, load_sem.at[10])
    table_copy.start()
    for s in range(3):
        sums_user[s, slots] = zero
        sums_item[s, slots] = zero
    for load in small_loads[2:]:
        load.wait()
    table_copy.wait()

    def compute(s):
        for t in range(tiles):
            flipped[t] = blocks[s][t].T
        count = counts[0, 0, s]

        def body(i, carry):
            base = i * GROUP
            held = []
            for g in range(GROUP):
                k = base + g
                u = users[user_tiles[s, 0, k]]
                it = item_tiles[s, 0, k]
                v = blocks[s][it]
                p = jnp.dot(u, flipped[it], preferred_element_type=F32)
                rating = rbuf[s, k].astype(F32)
                live = (k < count).astype(F32)
                e = ((1.0 + CONFIDENCE * rating) * (rating - p) * live).astype(BF16)
                held.append((k, u, v, e))
            for k, u, v, e in held:
                gu = jnp.dot(e, v, preferred_element_type=F32)
                gi = lax.dot_general(e, u, (((0,), (0,)), ((), ())), preferred_element_type=F32)
                sums_user[s, k] = gu + sums_user[s, table[s, k]]
                sums_item[s, k] = gi + sums_item[s, table[3 + s, k]]
            return carry

        lax.fori_loop(0, slots // GROUP, body, 0)

    def half_copy(s):
        return remote(half_out.at[s], half_in.at[s], half_sem, s, partner)

    def send_half(s):
        for t in range(tiles):
            end = table[3 + s, slots + t]
            rows = pl.ds(pl.multiple_of((1 - c) * half, half), half)
            half_out[s, t] = sums_item[s, end, rows].astype(BF16)
        half_copy(s).start()

    def piece_copy(s, e):
        return remote(
            chip_sum.at[s, pl.ds(target(e) * per, per)],
            pieces.at[s, e],
            piece_sem,
            s * nq + e,
            (col(1) if s == 1 else b, 2 * target(e) + c),
        )

    def outgoing(s):
        return by_distance + [0] if s == 1 else by_distance

    def send_pieces(s):
        half_copy(s).wait_recv()
        for e in outgoing(s) + ([] if s == 1 else [0]):
            for p in range(per):
                t = target(e) * per + p
                end = table[3 + s, slots + t]
                rows = pl.ds(pl.multiple_of(c * half, half), half)
                both = sums_item[s, end, rows] + half_in[s, t].astype(F32)
                chip_sum[s, t] = both.astype(BF16)
            if s == 1 or e > 0:
                piece_copy(s, e).start()

    def column_sum(s):
        for e in outgoing(s):
            piece_copy(s, e).wait_recv()
        total = None if s == 1 else chip_sum[s, pl.ds(q * per, per)].astype(F32)
        for e in outgoing(s):
            term = pieces[s, e].astype(F32)
            total = term if total is None else total + term
        return total

    def fwd_copy(s):
        return remote(fwd_out, fwd_in, fwd_sem, 0, (col(s), r))

    user_load.wait()
    item_load.wait()
    rating_load(0).wait()
    compute(0)
    send_half(0)

    for h in range(2):
        far_copy(h).wait_recv()
        swap_copy(2, h).start()

        @pl.when(yl == 0)
        def _():
            near_copy(h, block_2.at[part(h)]).start()

    send_pieces(0)
    for h in range(2):
        swap_copy(2, h).wait_recv()
    rating_load(2).wait()
    compute(2)
    send_half(2)

    for h in range(2):
        near_copy(h, items_hbm.at[part(h)]).wait_recv()
        swap_copy(1, h).start()
    send_pieces(2)
    for h in range(2):
        swap_copy(1, h).wait_recv()
    rating_load(1).wait()
    compute(1)
    send_half(1)

    for t in range(tiles):
        grad = zero
        for s in ORDER:
            grad = grad + sums_user[s, table[s, slots + t]]
        old = users[t].astype(F32)
        unew[t] = (old - rate_user * (grad + SHRINKAGE * old)).astype(BF16)
    user_store = pltpu.make_async_copy(unew, user_out, out_sem.at[0])
    user_store.start()

    send_pieces(1)
    fwd_out[...] = column_sum(2)
    fwd_copy(2).start()
    total = column_sum(0)
    fwd_copy(2).wait_recv()
    total = total + fwd_in[...]
    total = total + column_sum(1)

    mine = pl.ds(q * per, per)
    old = block_0[mine, pl.ds(pl.multiple_of(c * half, half), half)].astype(F32)
    inew[mine, c] = (old - rate_item * (total + SHRINKAGE * old)).astype(BF16)

    def gather_copy(e, cross=0):
        view = inew.at[mine, c]
        core = 1 - c if cross else c
        return remote(view, view, gather_sem, cross * nq + e, (b, 2 * target(e) + core))

    def gathered(e, cross=0):
        core = 1 - c if cross else c
        view = inew.at[pl.ds(source(e) * per, per), core]
        return remote(view, view, gather_sem, cross * nq + e, (b, 2 * target(e) + core))

    gathers = [(e, cross) for e in by_distance for cross in (0, 1)] + [(0, 1)]
    for e, cross in gathers:
        gather_copy(e, cross).start()
    for e, cross in reversed(gathers):
        gathered(e, cross).wait_recv()
    item_store = pltpu.make_async_copy(inew, item_out, out_sem.at[1])
    item_store.start()

    for h in range(2):
        far_copy(h).wait_send()
        near_copy(h, items_hbm.at[part(h)]).wait_send()
        for s in (1, 2):
            swap_copy(s, h).wait_send()
    for s in ORDER:
        half_copy(s).wait_send()
        for e in outgoing(s):
            piece_copy(s, e).wait_send()
    fwd_copy(2).wait_send()
    for e, cross in gathers:
        gather_copy(e, cross).wait_send()
    user_store.wait()
    item_store.wait()


def finish(user_new, item_new, user_out, item_out, sem):
    moves = [
        pltpu.make_async_copy(user_new, user_out, sem.at[0]),
        pltpu.make_async_copy(item_new, item_out, sem.at[1]),
    ]
    for move in moves:
        move.start()
    for move in moves:
        move.wait()


def on_device(users, items, ratings, user_tiles, item_tiles, counts):
    tile = ratings.shape[-1]
    rank = users.shape[1]
    stops, slots = ratings.shape[2:4]
    tiles = users.shape[0] // tile
    half = tile // 2
    nq = lax.axis_size("rep") // 2
    per = tiles // nq
    rate_user = STEP_GAIN / math.sqrt(stops * slots * tile * tile / users.shape[0])
    rate_item = STEP_GAIN / math.sqrt(2 * nq * stops * slots * tile * tile / items.shape[0])
    hbm = pl.BlockSpec(memory_space=pltpu.HBM)
    anywhere = pl.BlockSpec(memory_space=pl.ANY)
    dma = pltpu.SemaphoreType.DMA
    user_new, item_new = pl.pallas_call(
        functools.partial(kernel, rate_user, rate_item),
        out_shape=(
            pltpu.VMEM((tiles, tile, rank), BF16),
            pltpu.VMEM((tiles, 2, half, rank), BF16),
        ),
        in_specs=[hbm] * 6,
        out_specs=(anywhere, anywhere),
        scratch_shapes=[
            pltpu.VMEM((tiles, tile, rank), BF16),
            pltpu.VMEM((tiles, tile, rank), BF16),
            pltpu.VMEM((tiles, tile, rank), BF16),
            pltpu.VMEM((tiles, tile, rank), BF16),
            pltpu.VMEM((tiles, rank, tile), BF16),
            pltpu.VMEM((stops, slots, tile, tile), BF16),
            pltpu.VMEM((stops, slots + 1, tile, rank), F32),
            pltpu.VMEM((stops, slots + 1, tile, rank), F32),
            pltpu.VMEM((stops, tiles, half, rank), BF16),
            pltpu.VMEM((stops, tiles, half, rank), BF16),
            pltpu.VMEM((stops, tiles, half, rank), BF16),
            pltpu.VMEM((stops, nq, per, half, rank), BF16),
            pltpu.VMEM((per, half, rank), F32),
            pltpu.VMEM((per, half, rank), F32),
            pltpu.VMEM((tiles, tile, rank), BF16),
            pltpu.VMEM((tiles, 2, half, rank), BF16),
            pltpu.SMEM((stops, 1, slots), jnp.int32),
            pltpu.SMEM((stops, 1, slots), jnp.int32),
            pltpu.SMEM((1, 1, stops), jnp.int32),
            pltpu.VMEM((2, stops, 1, slots), jnp.int32),
            pltpu.VMEM((8, 128), jnp.int32),
            pltpu.VMEM((8, 128), jnp.int32),
            pltpu.SMEM((8, 128), jnp.int32),
            dma((11,)),
            dma((2, 4)),
            dma((2, 4)),
            dma((2, 3)),
            dma((2, 3 * nq)),
            dma((2, 1)),
            dma((2, 2 * nq)),
            dma((2,)),
        ],
        compiler_params=pltpu.CompilerParams(
            collective_id=0, has_side_effects=True, vmem_limit_bytes=60000000
        ),
    )(
        user_tiles.reshape(stops, 1, slots),
        item_tiles.reshape(stops, 1, slots),
        counts,
        users.reshape(tiles, tile, rank),
        items.reshape(tiles, tile, rank),
        ratings[0, 0],
    )
    user_new = user_new.reshape(users.shape)
    item_new = item_new.reshape(items.shape)
    return pl.pallas_call(
        finish,
        out_shape=(
            jax.ShapeDtypeStruct(users.shape, BF16),
            jax.ShapeDtypeStruct(items.shape, BF16),
        ),
        in_specs=[pl.BlockSpec(memory_space=pltpu.VMEM)] * 2,
        out_specs=(anywhere, anywhere),
        scratch_shapes=[dma((2,))],
        compiler_params=pltpu.CompilerParams(vmem_limit_bytes=4 << 20),
    )(user_new, item_new)


def solution(mesh):
    return jax.shard_map(
        on_device,
        mesh=mesh,
        in_specs=(
            P(("blk", "rep"), None),
            P("blk", None),
            P("blk", "rep", None, None, None, None),
            P("blk", "rep", None, None),
            P("blk", "rep", None, None),
            P("blk", "rep", None),
        ),
        out_specs=(P(("blk", "rep"), None), P("blk", None)),
        check_vma=False,
    )
```
